32 devices in a mesh: tm: 8 (over z, y), order: 4 (over x, core).
Axes of the slice: x: 2, y: 2, z: 4, core: 2. Of those that a mesh axis runs over, the one named last changes fastest.
Arguments:
- design: bfloat16 [3, 1024, 65536], P(None, 'tm', 'order'), may hold values from -0.109375 to 0.109375
- gap_flags: int32 [1024], P('tm'), may hold values 0 or 1
- segment_ids: int32 [1024], P('tm'), may hold values from 0 to 3, never falling along the last dimension, each value on 1 to 512 neighbouring positions
- ar_order: int32 [3], replicated, may hold values from 1 to 4
- ma_order: int32 [3], replicated, may hold values from 1 to 4
- ar_roots: float32 [3, 4], replicated, may hold values from -0.5 to 1, as said below
- ma_roots: float32 [3, 4], replicated, may hold values from -0.5 to 1, as said below
- kaula: float32 [4, 16384], P('order', 'tm'), may hold values from 0.2 to 2
- precond: float32 [4, 128, 128, 128], P('order', 'tm'), as said below
- solution: float32 [16, 4, 16384], P(None, 'order', 'tm'), may hold values from -6 to 6
- residual: float32 [16, 4, 16384], P(None, 'order', 'tm'), may hold values from -6 to 6
- direction: float32 [16, 4, 16384], P(None, 'order', 'tm'), may hold values from -6 to 6
Outputs:
- new_solution: float32 [16, 4, 16384], P(None, 'order', 'tm')
- new_residual: float32 [16, 4, 16384], P(None, 'order', 'tm')
- new_direction: float32 [16, 4, 16384], P(None, 'order', 'tm')
The draws below stay inside these ranges and needn't reach their ends.
Inputs may be any that keep to these rules, and one draw needn't show every extreme that they name: The first root of each component of ar_roots lies within 2 / 1024 below 1; the others lie within 0.5 of zero. The first root of each component of ma_roots lies within 12 / 1024 below 1; the others lie within 0.5 of zero. `precond`: every block is symmetric positive definite.
All inputs are finite; a program needn't handle non-finite values. No bound on the sum of `gap_flags` on one device may be relied on, other than what follows from the above.
Results may differ from the reference program's by a relative error of at most 0.0036.
Values may be sent and summed in bfloat16 or wider, within the bound.
A program may use at most 64 MiB of HBM per device.

```python
import math
import jax
import jax.numpy as jnp
import numpy as np
from jax import lax

NCOEF = 65536
BLK = 128
PMAX = 4
QMAX = 4
SEGMENTS = 4
NRHS = 16
EPOCHS = 1024
CD = 16384
BLOCKS_O = 128
N_ORDER = 4


def draw_ar_roots(key, part):
    lead_key, rest_key = jax.random.split(jax.random.fold_in(key, 11))
    spread = jax.random.uniform(lead_key, (3,), jnp.float32, 0.5, 2.0)
    leading = 1.0 - spread / EPOCHS
    others = jax.random.uniform(rest_key, (3, PMAX - 1), jnp.float32, -0.5, 0.5)
    return jnp.concatenate([leading[:, None], others], axis=1)


def draw_ma_roots(key, part):
    lead_key, rest_key = jax.random.split(jax.random.fold_in(key, 23))
    spread = jax.random.uniform(lead_key, (3,), jnp.float32, 1.0, 3.0)
    leading = 1.0 - 4.0 * spread / EPOCHS
    others = jax.random.uniform(rest_key, (3, QMAX - 1), jnp.float32, -0.5, 0.5)
    return jnp.concatenate([leading[:, None], others], axis=1)


def draw_precond(key, part):
    off_key, diag_key = jax.random.split(jax.random.fold_in(key, 37), 2)
    raw = jax.random.normal(off_key, (N_ORDER, BLOCKS_O, BLK, BLK), jnp.float32) / BLK
    symmetric = raw + jnp.swapaxes(raw, 2, 3)
    identity = jnp.eye(BLK, dtype=jnp.float32)
    off_diag = symmetric * (1.0 - identity)
    extra = jax.random.uniform(diag_key, (N_ORDER, BLOCKS_O, BLK), jnp.float32, 0.1, 1.0)
    diagonal = 1.25 * jnp.sum(jnp.abs(off_diag), axis=3) + extra
    matrix = off_diag + diagonal[..., None] * identity
    return matrix


def set_ends(values, key, low, top_value):
    dims = values.shape
    place = [jax.random.randint(jax.random.fold_in(key, axis), (), 0, dims[axis]) for axis in range(len(dims))]
    values = values.at[tuple(place)].set(low)
    longest = dims.index(max(dims))
    place[longest] = (place[longest] + 1) % dims[longest]
    return values.at[tuple(place)].set(top_value)


def levels(stream_key, dims, cuts, low, top_value):
    loudness = 1.0
    for axis_at, shards_of in cuts:
        steps = jax.random.uniform(jax.random.fold_in(jax.random.fold_in(stream_key, 6), axis_at), (shards_of,), jnp.float32, low / len(cuts), top_value / len(cuts))
        loudness = loudness * jnp.repeat(jnp.exp(steps), dims[axis_at] // shards_of).reshape((-1,) + (1,) * (len(dims) - 1 - axis_at))
    return loudness


def split_up(count, total, most, skew):
    weights = [(1 << 20) // math.isqrt(rank ** skew) + 1 for rank in range(2, count + 1)]
    spare, holding = total - most - (count - 1), [1] * (count - 1)
    while spare > 0:
        movable = [i for i in range(count - 1) if holding[i] < most]
        whole, remaining = sum([weights[i] for i in movable]), spare
        for i in movable:
            more = min(most - holding[i], max(1, remaining * weights[i] // whole), spare)
            holding[i] = holding[i] + more
            spare = spare - more
    return np.array([most] + holding)


def uneven(own_key, number_of, total, limit, slope):
    if number_of == 2:
        one = jax.random.randint(own_key, (), max(1, total - limit), min(limit, total - 1) + 1)
        return jnp.stack([one, total - one])
    tallies = jnp.asarray(split_up(number_of, total, limit, slope), jnp.int32)
    pairs = (number_of - 1) // 2
    source_of, sink = tallies[1:1 + 2 * pairs:2], tallies[2:2 + 2 * pairs:2]
    slack = jnp.minimum(source_of - 1, limit - sink)
    moved = jax.random.randint(jax.random.fold_in(own_key, 1), (pairs,), 0, 1 << 20) % (slack + 1)
    tallies = tallies.at[1:1 + 2 * pairs:2].set(source_of - moved).at[2:2 + 2 * pairs:2].set(sink + moved)
    return tallies[jax.random.permutation(jax.random.fold_in(own_key, 2), number_of)]


def scatter_about(own_key, extent, scale, reach, cuts=(), kind=jnp.bfloat16):
    gain = levels(own_key, extent, cuts, -0.22, 0.18) if cuts else 1.0
    entries = jax.random.normal(own_key, extent, jnp.float32) * scale * gain
    return jnp.minimum(jnp.maximum(entries, -reach), reach).astype(kind)


def setup_inputs(seed: int = 0) -> dict:
    seeds = jax.random.split(jax.random.key(seed), 13)
    design = scatter_about(seeds[0], (3, EPOCHS, NCOEF), (3 * EPOCHS) ** -0.5, 0.109375, ((1, 8), (2, 4)))
    gap_flags = set_ends((jax.random.randint(seeds[1], (EPOCHS,), 0, 16) < 15).astype(jnp.int32), jax.random.fold_in(seeds[1], 1), 0, 1)
    segment_ids = jnp.searchsorted(jnp.cumsum(uneven(seeds[2], SEGMENTS, EPOCHS, EPOCHS // 2, 0)), jnp.arange(EPOCHS), side="right").astype(jnp.int32)
    ar_order = jax.random.randint(seeds[3], (3,), 1, PMAX + 1).astype(jnp.int32)
    ma_order = jax.random.randint(seeds[4], (3,), 1, QMAX + 1).astype(jnp.int32)
    ar_roots = draw_ar_roots(jax.random.fold_in(seeds[12], 71), 0)
    ma_roots = draw_ma_roots(jax.random.fold_in(seeds[12], 71), 0)
    kaula = jnp.clip(jnp.exp(math.log(2.0) - 2.3025851 * jax.random.uniform(seeds[7], (N_ORDER, CD), jnp.float32) ** levels(seeds[7], (N_ORDER, CD), ((0, 4), (1, 8)), -0.2, 0.2)), 0.2, 2.0)
    precond = draw_precond(jax.random.fold_in(seeds[12], 71), 0)
    solution = scatter_about(seeds[9], (NRHS, N_ORDER, CD), 1.0, 6.0, ((1, 4), (2, 8)), jnp.float32)
    residual = scatter_about(seeds[10], (NRHS, N_ORDER, CD), 1.0, 6.0, ((1, 4), (2, 8)), jnp.float32)
    direction = scatter_about(seeds[11], (NRHS, N_ORDER, CD), 1.0, 6.0, ((1, 4), (2, 8)), jnp.float32)
    return {"design": design, "gap_flags": gap_flags, "segment_ids": segment_ids, "ar_order": ar_order, "ma_order": ma_order, "ar_roots": ar_roots, "ma_roots": ma_roots, "kaula": kaula, "precond": precond, "solution": solution, "residual": residual, "direction": direction}


def polynomial(root_values, filter_order):
    number_roots = root_values.shape[1]
    coeffs = jnp.concatenate([jnp.ones((3, 1), root_values.dtype), jnp.zeros((3, number_roots), root_values.dtype)], axis=1)
    for position in range(number_roots):
        active = jnp.where(position < filter_order, root_values[:, position], jnp.zeros_like(root_values[:, position]))
        lagged = jnp.concatenate([jnp.zeros_like(coeffs[:, :1]), coeffs[:, :-1]], axis=1)
        coeffs = coeffs - active[:, None] * lagged
    return coeffs


def moving_part(series, coeffs, seg_ids, backward):
    length = series.shape[2]
    total = jnp.zeros_like(series)
    for lag_step in range(coeffs.shape[1]):
        if backward:
            moved = jnp.pad(series, ((0, 0), (0, 0), (0, lag_step)))[:, :, lag_step:]
            moved_ids = jnp.pad(seg_ids, (0, lag_step), constant_values=-1)[lag_step:]
        else:
            moved = jnp.pad(series, ((0, 0), (0, 0), (lag_step, 0)))[:, :, :length]
            moved_ids = jnp.pad(seg_ids, (lag_step, 0), constant_values=-1)[:length]
        joined = (moved_ids == seg_ids)[None, None, :]
        total = total + coeffs[:, lag_step][None, :, None] * jnp.where(joined, moved, jnp.zeros_like(moved))
    return total


def recursive_part(series, coeffs, seg_ids, backward):
    lags = coeffs.shape[1] - 1
    weights = coeffs[:, 1:].T[:, None, :]

    def advance(carry, inputs):
        buffer, id_buffer = carry
        value, current = inputs
        joined = (id_buffer == current)[:, None, None]
        coupling = jnp.sum(jnp.where(joined, weights * buffer, jnp.zeros_like(buffer)), axis=0)
        result = value - coupling
        new_buffer = jnp.concatenate([result[None], buffer[:-1]], axis=0)
        new_ids = jnp.concatenate([current[None], id_buffer[:-1]], axis=0)
        return (new_buffer, new_ids), result

    start = (jnp.zeros((lags,) + series.shape[:2], series.dtype), jnp.full((lags,), -1, jnp.int32))
    _, outputs = lax.scan(advance, start, (jnp.moveaxis(series, 2, 0), seg_ids), reverse=backward)
    return jnp.moveaxis(outputs, 0, 2)


def precondition(blocks, vector):
    rows = vector.shape[0]
    shaped = vector.reshape(rows, blocks.shape[0], blocks.shape[1])
    return jnp.einsum("bij,rbj->rbi", blocks, shaped, precision=lax.Precision.HIGHEST).reshape(rows, -1)


def reference(design, gap_flags, segment_ids, ar_order, ma_order, ar_roots, ma_roots, kaula, precond, solution, residual, direction):
    rhs_count = direction.shape[0]
    epochs = design.shape[1]
    columns = design.shape[2]
    flat_dir = direction.reshape(rhs_count, columns)
    flat_res = residual.reshape(rhs_count, columns)
    flat_sol = solution.reshape(rhs_count, columns)
    flat_kaula = kaula.reshape(columns)
    blocks = precond.reshape(-1, precond.shape[2], precond.shape[3])
    design_flat = design.reshape(3 * epochs, columns)
    packed = flat_dir.astype(jnp.bfloat16)
    observed = lax.dot_general(packed, design_flat, (((1,), (1,)), ((), ())), preferred_element_type=jnp.float32)
    observed = observed.reshape(rhs_count, 3, epochs)
    gaps = gap_flags.astype(observed.dtype)
    ar_coeffs = polynomial(ar_roots, ar_order)
    ma_coeffs = polynomial(ma_roots, ma_order)
    masked = observed * gaps[None, None, :]
    moving = moving_part(masked, ma_coeffs, segment_ids, False)
    filtered = recursive_part(moving, ar_coeffs, segment_ids, False)
    adjoint = recursive_part(filtered, ar_coeffs, segment_ids, True)
    weighted = (moving_part(adjoint, ma_coeffs, segment_ids, True) * gaps[None, None, :]).astype(jnp.bfloat16)
    gradient = jnp.dot(weighted.reshape(rhs_count, 3 * epochs), design_flat, preferred_element_type=jnp.float32)
    image = gradient + flat_kaula[None, :] * flat_dir
    applied = precondition(blocks, flat_res)
    old_rz = jnp.sum(flat_res * applied, axis=1)
    curvature = jnp.sum(flat_dir * image, axis=1)
    step_len = (old_rz / curvature)[:, None]
    new_solution = flat_sol + step_len * flat_dir
    new_residual = flat_res - step_len * image
    new_applied = precondition(blocks, new_residual)
    new_rz = jnp.sum(new_residual * new_applied, axis=1)
    new_direction = new_applied + (new_rz / old_rz)[:, None] * flat_dir
    shape = direction.shape
    return new_solution.reshape(shape), new_residual.reshape(shape), new_direction.reshape(shape)
```

```python
import functools

import jax
import jax.numpy as jnp
from jax import lax
from jax.experimental import pallas as pl
from jax.experimental.pallas import tpu as pltpu
from jax.sharding import PartitionSpec as P

LINK = jnp.float32
LAGS = 4
HI = lax.Precision.HIGHEST
NN = (((1,), (0,)), ((), ()))
NT = (((1,), (1,)), ((), ()))


def dot(a, b, dims, precision=None):
    return lax.dot_general(a, b, dims, precision=precision, preferred_element_type=jnp.float32)


def rows_of(pieces, count, width):
    row = lax.broadcasted_iota(jnp.int32, (count, width), 0)
    out = jnp.zeros((count, width), jnp.float32)
    for at, piece in pieces:
        out = jnp.where(row == at, piece, out)
    return out


def tall(block, rows):
    return jnp.concatenate(
        [block, jnp.zeros((rows - block.shape[0], block.shape[1]), jnp.float32)], axis=0
    )


def bands(matrix):
    row = lax.broadcasted_iota(jnp.int32, matrix.shape, 0)
    col = lax.broadcasted_iota(jnp.int32, matrix.shape, 1)
    inside = row // LAGS == col // LAGS
    return [
        jnp.sum(
            jnp.where(inside & (row == col - shift), matrix, 0.0), axis=0, keepdims=True
        )
        for shift in range(1 - LAGS, LAGS)
    ]


def banded(vector, coeffs):
    width = vector.shape[1]
    total = None
    for shift, coeff in zip(range(1 - LAGS, LAGS), coeffs):
        moved = vector if shift == 0 else pltpu.roll(vector, shift % width, 1)
        total = moved * coeff if total is None else total + moved * coeff
    return total


def filters(ar_ref, ma_ref, aro_ref, mao_ref, ids, pt_ref):
    n = ids.shape[1]
    lane = lax.broadcasted_iota(jnp.int32, (1, n), 1)

    def lagged(v, k):
        return v if k == 0 else jnp.where(lane >= k, pltpu.roll(v, k, 1), 0.0)

    impulse = jnp.where(lane == 0, 1.0, 0.0).astype(jnp.float32)
    grid = jnp.broadcast_to(ids, (n, n))
    row = lax.broadcasted_iota(jnp.int32, (n, n), 0)
    col = lax.broadcasted_iota(jnp.int32, (n, n), 1)
    joined = (grid == grid.T) & (col >= row)
    out_rows, in_rows, end_rows = [], [], []
    for c in range(3):
        ar = [jnp.where(k < aro_ref[c], ar_ref[c, k], 0.0) for k in range(LAGS)]
        ma = [jnp.where(k < mao_ref[c], ma_ref[c, k], 0.0) for k in range(LAGS)]
        a, b = [1.0] + [0.0] * LAGS, [1.0] + [0.0] * LAGS
        for k in range(LAGS):
            a = [a[0]] + [a[j] - ar[k] * a[j - 1] for j in range(1, LAGS + 1)]
            b = [b[0]] + [b[j] - ma[k] * b[j - 1] for j in range(1, LAGS + 1)]
        h = impulse
        for k in range(LAGS):
            power, m = ar[k], 1
            while m < n:
                h = h + power * lagged(h, m)
                power, m = power * power, 2 * m
        g = h
        for k in range(LAGS):
            g = g - ma[k] * lagged(g, 1)
        for i in range(1, LAGS + 1):
            out_rows.append((c * LAGS + i - 1, lagged(h, i - 1)))
            acc = jnp.zeros_like(g)
            end = jnp.zeros_like(g)
            for m in range(LAGS + 1 - i):
                acc = acc + b[i + m] * lagged(impulse, m) - a[i + m] * lagged(g, m)
                end = end - a[i + m] * jnp.where(lane == n - 1 - m, 1.0, 0.0)
            in_rows.append((c * LAGS + i - 1, acc))
            end_rows.append((c * LAGS + i - 1, end))
        t = jnp.broadcast_to(g, (n, n))
        bit = 1
        while bit < n:
            t = jnp.where((row // bit) % 2 == 1, pltpu.roll(t, bit, 1), t)
            bit *= 2
        pt_ref[c] = jnp.where(joined, t, 0.0)
    ca = rows_of(out_rows, 16, n)
    flip = jnp.where(row + col == n - 1, 1.0, 0.0).astype(jnp.float32)
    ab = dot(rows_of(in_rows, 16, n), flip, NN, HI)
    ends = rows_of(end_rows, 16, n)
    fwd = bands(dot(ca, tall(ends, n), NT, HI))
    bwd = bands(dot(ends, tall(ca, n), NT, HI))
    return ca, ab, fwd, bwd


def spread(block, mask):
    row = lax.broadcasted_iota(jnp.int32, block.shape, 0)
    return jnp.concatenate(
        [jnp.where(row // LAGS == c, block * mask, 0.0) for c in range(3)], axis=1
    )


def kernel(
    T, O,
    design, packed, ids_in, gaps, ar_ref, ma_ref, aro_ref, mao_ref, kaula, precond,
    sol, res, direc,
    new_sol, new_res, new_dir,
    dv, right_in, left_in, obs_out, obs_in, ids_all, summ_out, summ_in, pt,
    rs_right_out, rs_left_out, rs_right_in, rs_left_in, applied, image_applied,
    tot_out, tot_in, tot2_out, tot2_in,
    dsem, agr_s, agr_r, agl_s, agl_r, ob_s, ob_r, id_s, id_r, su_s, su_r,
    rr_s, rr_r, rl_s, rl_r, t1_s, t1_r, t2_s, t2_r,
):
    me, order = lax.axis_index("tm"), lax.axis_index("order")
    A = T // 2
    share = packed.shape[1]
    n = ids_in.shape[1]
    right_n, left_n = T // 2, T - 1 - T // 2

    def tm_at(p):
        p = lax.rem(p + 2 * T, T)
        return jnp.where(p < A, 2 * p, 2 * (T - 1 - p) + 1)

    pos = jnp.where(me % 2 == 0, me // 2, T - 1 - me // 2)
    right, left = {"tm": tm_at(pos + 1)}, {"tm": tm_at(pos - 1)}

    def to_tm(k):
        return {"tm": lax.rem(me + k, T)}

    def to_order(k):
        return {"order": lax.rem(order + k, O)}

    def load(dist):
        q = tm_at(pos + dist)
        return pltpu.make_async_copy(
            design.at[:, pl.ds(pl.multiple_of(q * share, 128), share)],
            dv.at[dist % T],
            dsem.at[dist % T],
        )

    def remote(src, dst, ssem, rsem, to):
        return pltpu.make_async_remote_copy(
            src_ref=src, dst_ref=dst, send_sem=ssem, recv_sem=rsem,
            device_id=to, device_id_type=pl.DeviceIdType.MESH,
        )

    arrivals = [0]
    for s in range(1, right_n + 1):
        arrivals.append(-s)
        if s <= left_n:
            arrivals.append(s)
    for dist in arrivals:
        load(dist).start()

    barrier = pltpu.get_barrier_semaphore()
    for k in range(1, T):
        pl.semaphore_signal(barrier, inc=1, device_id=to_tm(k), device_id_type=pl.DeviceIdType.MESH)
    for k in range(1, O):
        pl.semaphore_signal(barrier, inc=1, device_id=to_order(k), device_id_type=pl.DeviceIdType.MESH)
    pl.semaphore_wait(barrier, T - 1 + O - 1)

    def ag_right(s):
        src = packed if s == 0 else right_in.at[s - 1]
        return remote(src, right_in.at[s], agr_s.at[s], agr_r.at[s], right)

    def ag_left(s):
        src = packed if s == 0 else left_in.at[s - 1]
        return remote(src, left_in.at[s], agl_s.at[s], agl_r.at[s], left)

    ag_right(0).start()
    ag_left(0).start()
    id_copies = [
        remote(ids_in, ids_all.at[k - 1], id_s.at[k - 1], id_r.at[k - 1], to_tm(k))
        for k in range(1, T)
    ]
    for copy in id_copies:
        copy.start()

    load(0).wait()
    obs = dot(packed[...], dv[0], NT)
    ids = ids_in[0:1, :]
    ca, ab, fwd, bwd = filters(ar_ref, ma_ref, aro_ref, mao_ref, ids, pt)
    for s in range(right_n):
        ag_right(s).wait_recv()
        if s + 1 < right_n:
            ag_right(s + 1).start()
        if s < left_n:
            ag_left(s).wait_recv()
            if s + 1 < left_n:
                ag_left(s + 1).start()
        load(-(s + 1)).wait()
        obs = obs + dot(right_in[s], dv[(-(s + 1)) % T], NT)
        if s < left_n:
            load(s + 1).wait()
            obs = obs + dot(left_in[s], dv[s + 1], NT)
    obs_out[...] = obs
    ob_copies = [
        remote(obs_out, obs_in.at[k - 1], ob_s.at[k - 1], ob_r.at[k - 1], to_order(k))
        for k in range(1, O)
    ]
    for copy in ob_copies:
        copy.start()

    first, last = ids[:, 0:1], ids[:, n - 1 : n]
    at_first = jnp.where(ids == first, 1.0, 0.0)
    at_last = jnp.where(ids == last, 1.0, 0.0)
    head_map = spread(ca, at_first)
    tail_map = spread(ab, at_last)
    head16 = tall(head_map, n)
    tail16 = tall(tail_map, n)
    zeros64 = jnp.zeros((n // 2, 3 * n), jnp.float32)
    head_low = jnp.concatenate([zeros64, head16[: n // 2]], axis=0)
    for copy in id_copies:
        copy.wait_recv()
    ids_e = []
    for e in range(T):
        slot = lax.rem(me - e + T - 1, T)
        slot = jnp.minimum(slot, T - 2)
        ids_e.append(jnp.where(me == e, ids, ids_all[slot][0:1, :]))
    firsts = [v[:, 0:1] for v in ids_e]
    lasts = [v[:, n - 1 : n] for v in ids_e]
    runs = jnp.concatenate(
        [ca * jnp.where(v == f, 1.0, 0.0) for v, f in zip(ids_e, firsts)], axis=0
    )
    energy = dot(runs, tall(ca, n), NT, HI)
    energies = [bands(energy[16 * e : 16 * e + 16]) for e in range(T)]

    for copy in ob_copies:
        copy.wait_recv()
    for k in range(1, O):
        obs = obs + obs_in[k - 1]
    gaps3 = jnp.concatenate([gaps[0:1, :]] * 3, axis=1)
    masked = obs * gaps3
    local = jnp.concatenate(
        [dot(masked[:, c * n : (c + 1) * n], pt[c], NN, HI) for c in range(3)], axis=1
    )
    summary = dot(masked, tail16, NT, HI) + dot(local, head_low, NT, HI)
    summ_out[...] = summary
    su_copies = [
        remote(summ_out, summ_in.at[k - 1], su_s.at[k - 1], su_r.at[k - 1], to_tm(k))
        for k in range(1, T)
    ]
    for copy in su_copies:
        copy.start()
    local_back = jnp.concatenate(
        [dot(local[:, c * n : (c + 1) * n], pt[c], NT, HI) for c in range(3)], axis=1
    )
    for copy in su_copies:
        copy.wait_recv()
    sums = []
    for e in range(T):
        slot = jnp.minimum(lax.rem(me - e + T - 1, T), T - 2)
        sums.append(jnp.where(me == e, summary, summ_in[slot]))
    state = jnp.zeros_like(summary)
    mine_in = jnp.zeros_like(summary)
    ins = []
    for e in range(T):
        entering = state if e == 0 else state * jnp.where(lasts[e - 1] == firsts[e], 1.0, 0.0)
        ins.append(entering)
        mine_in = jnp.where(me == e, entering, mine_in)
        through = jnp.where(firsts[e] == lasts[e], 1.0, 0.0)
        state = sums[e] + through * banded(entering, fwd)
    back = jnp.zeros_like(summary)
    mine_back = jnp.zeros_like(summary)
    for e in range(T - 1, 0, -1):
        through = jnp.where(firsts[e] == lasts[e], 1.0, 0.0)
        heads = pltpu.roll(sums[e], n // 2, 1) + banded(ins[e], energies[e])
        back = (heads + through * banded(back, bwd)) * jnp.where(
            lasts[e - 1] == firsts[e], 1.0, 0.0
        )
        mine_back = jnp.where(me == e - 1, back, mine_back)
    lane = lax.broadcasted_iota(jnp.int32, summary.shape, 1)
    mine_in = jnp.where(lane < 3 * LAGS, mine_in, 0.0)
    mine_back = jnp.where(lane < 3 * LAGS, mine_back, 0.0)
    entered = dot(mine_in, head16, NN, HI)
    entered_back = jnp.concatenate(
        [dot(entered[:, c * n : (c + 1) * n], pt[c], NT, HI) for c in range(3)], axis=1
    )
    adjoint = local_back + entered_back + dot(mine_back, tail16, NN, HI)
    weighted = (adjoint * gaps3).astype(jnp.bfloat16)

    def grad(dist):
        return dot(weighted, dv[dist % T], NN)

    def rs_right(s):
        return remote(rs_right_out.at[s], rs_right_in.at[s], rr_s.at[s], rr_r.at[s], right)

    def rs_left(s):
        return remote(rs_left_out.at[s], rs_left_in.at[s], rl_s.at[s], rl_r.at[s], left)

    for s in range(right_n):
        piece = grad(right_n - s)
        if s > 0:
            rs_right(s - 1).wait_recv()
            piece = piece + rs_right_in[s - 1].astype(jnp.float32)
        rs_right_out[s] = piece.astype(LINK)
        rs_right(s).start()
        if s < left_n:
            piece = grad(s - left_n)
            if s > 0:
                rs_left(s - 1).wait_recv()
                piece = piece + rs_left_in[s - 1].astype(jnp.float32)
            rs_left_out[s] = piece.astype(LINK)
            rs_left(s).start()
    own = grad(0)
    blocks = precond.shape[0]
    for m in range(blocks):
        cols = slice(m * 128, (m + 1) * 128)
        applied[:, cols] = dot(res[:, cols], precond[m], NT, HI)
    rs_right(right_n - 1).wait_recv()
    own = own + rs_right_in[right_n - 1].astype(jnp.float32)
    if left_n > 0:
        rs_left(left_n - 1).wait_recv()
        own = own + rs_left_in[left_n - 1].astype(jnp.float32)
    image = own + kaula[...] * direc[...]
    for m in range(blocks):
        cols = slice(m * 128, (m + 1) * 128)
        image_applied[:, cols] = dot(image[:, cols], precond[m], NT, HI)
    app, imapp = applied[...], image_applied[...]
    d, r = direc[...], res[...]
    rhs = d.shape[0]
    lane = lax.broadcasted_iota(jnp.int32, (rhs, 128), 1)
    row = lax.broadcasted_iota(jnp.int32, (rhs, 128), 0)
    products = [r * app, d * image, image * app, image * imapp]
    total = jnp.zeros((rhs, 128), jnp.float32)
    for q, product in enumerate(products):
        total = jnp.where(lane == q * rhs + row, jnp.sum(product, axis=1, keepdims=True), total)
    total = jnp.broadcast_to(jnp.sum(total, axis=0, keepdims=True), (8, 128))

    def gather_sum(value, out, into, ssem, rsem, count, to):
        out[...] = value
        copies = [
            remote(out, into.at[k - 1], ssem.at[k - 1], rsem.at[k - 1], to(k))
            for k in range(1, count)
        ]
        for copy in copies:
            copy.start()
        for k, copy in enumerate(copies):
            copy.wait_recv()
            value = value + into[k]
        return value, copies

    total, c1 = gather_sum(total, tot_out, tot_in, t1_s, t1_r, O, to_order)
    total, c2 = gather_sum(total, tot2_out, tot2_in, t2_s, t2_r, T, to_tm)
    wide = jnp.broadcast_to(total[0:1, :], (rhs, 128))
    old_rz, curvature, cross, quad = [
        jnp.sum(jnp.where(lane == q * rhs + row, wide, 0.0), axis=1, keepdims=True)
        for q in range(4)
    ]
    step = old_rz / curvature
    new_rz = old_rz - 2.0 * step * cross + step * step * quad
    new_sol[...] = sol[...] + step * d
    new_res[...] = r - step * image
    new_dir[...] = app - step * imapp + (new_rz / old_rz) * d

    for s in range(right_n):
        ag_right(s).wait_send()
        rs_right(s).wait_send()
    for s in range(left_n):
        ag_left(s).wait_send()
        rs_left(s).wait_send()
    for copy in id_copies + ob_copies + su_copies + c1 + c2:
        copy.wait_send()


def on_device(
    T, O, design, gap_flags, segment_ids, ar_order, ma_order, ar_roots, ma_roots,
    kaula, precond, solution, residual, direction,
):
    n = segment_ids.shape[0]
    columns = design.shape[2]
    share = direction.shape[2]
    rhs = direction.shape[0]
    f32, bf16 = jnp.float32, jnp.bfloat16
    flat = lambda v: v.reshape(rhs, share)
    ids8 = jnp.broadcast_to(segment_ids.astype(f32)[None, :], (8, n))
    gaps8 = jnp.broadcast_to(gap_flags.astype(f32)[None, :], (8, n))
    packed = flat(direction).astype(bf16)
    right_n, left_n = T // 2, T - 1 - T // 2
    vmem = pl.BlockSpec(memory_space=pltpu.VMEM)
    smem = pl.BlockSpec(memory_space=pltpu.SMEM)
    V, D = pltpu.VMEM, lambda k: pltpu.SemaphoreType.DMA((max(k, 1),))
    L = max(left_n, 1)
    outs = pl.pallas_call(
        functools.partial(kernel, T, O),
        out_shape=[jax.ShapeDtypeStruct((rhs, share), f32)] * 3,
        in_specs=[pl.BlockSpec(memory_space=pl.ANY), vmem, vmem, vmem, smem, smem, smem, smem,
                  vmem, vmem, vmem, vmem, vmem],
        out_specs=[vmem] * 3,
        scratch_shapes=[
            V((T, 3 * n, share), bf16), V((right_n, rhs, share), bf16), V((L, rhs, share), bf16),
            V((rhs, 3 * n), f32), V((O - 1, rhs, 3 * n), f32), V((T - 1, 8, n), f32),
            V((rhs, n), f32), V((T - 1, rhs, n), f32), V((3, n, n), f32),
            V((right_n, rhs, share), LINK), V((L, rhs, share), LINK),
            V((right_n, rhs, share), LINK), V((L, rhs, share), LINK),
            V((rhs, share), f32), V((rhs, share), f32),
            V((8, 128), f32), V((O - 1, 8, 128), f32), V((8, 128), f32), V((T - 1, 8, 128), f32),
            D(T), D(right_n), D(right_n), D(L), D(L), D(O - 1), D(O - 1), D(T - 1), D(T - 1),
            D(T - 1), D(T - 1), D(right_n), D(right_n), D(L), D(L), D(O - 1), D(O - 1),
            D(T - 1), D(T - 1),
        ],
        compiler_params=pltpu.CompilerParams(
            collective_id=0, has_side_effects=True, vmem_limit_bytes=56 * 1024 * 1024
        ),
    )(
        design.reshape(3 * n, columns), packed, ids8, gaps8, ar_roots, ma_roots, ar_order,
        ma_order, kaula, precond[0], flat(solution), flat(residual), flat(direction),
    )
    return tuple(v.reshape(direction.shape) for v in outs)


def solution(mesh):
    vec = P(None, "order", "tm")
    in_specs = (
        P(None, "tm", "order"), P("tm"), P("tm"), P(), P(), P(), P(), P("order", "tm"),
        P("order", "tm", None, None), vec, vec, vec,
    )
    body = functools.partial(on_device, mesh.shape["tm"], mesh.shape["order"])
    return jax.shard_map(
        body, mesh=mesh, in_specs=in_specs, out_specs=(vec, vec, vec), check_vma=False
    )
```

```python
import functools

import jax
import jax.numpy as jnp
from jax import lax
from jax.experimental import pallas as pl
from jax.experimental.pallas import tpu as pltpu
from jax.sharding import PartitionSpec as P

LINK = jnp.bfloat16
LAGS = 4
HI = lax.Precision.HIGHEST
NN = (((1,), (0,)), ((), ()))
NT = (((1,), (1,)), ((), ()))


def dot(a, b, dims, precision=None):
    return lax.dot_general(a, b, dims, precision=precision, preferred_element_type=jnp.float32)


def rows_of(pieces, count, width):
    row = lax.broadcasted_iota(jnp.int32, (count, width), 0)
    out = jnp.zeros((count, width), jnp.float32)
    for at, piece in pieces:
        out = jnp.where(row == at, piece, out)
    return out


def tall(block, rows):
    return jnp.concatenate(
        [block, jnp.zeros((rows - block.shape[0], block.shape[1]), jnp.float32)], axis=0
    )


def bands(matrix):
    row = lax.broadcasted_iota(jnp.int32, matrix.shape, 0)
    col = lax.broadcasted_iota(jnp.int32, matrix.shape, 1)
    inside = row // LAGS == col // LAGS
    return [
        jnp.sum(
            jnp.where(inside & (row == col - shift), matrix, 0.0), axis=0, keepdims=True
        )
        for shift in range(1 - LAGS, LAGS)
    ]


def banded(vector, coeffs):
    width = vector.shape[1]
    total = None
    for shift, coeff in zip(range(1 - LAGS, LAGS), coeffs):
        moved = vector if shift == 0 else pltpu.roll(vector, shift % width, 1)
        total = moved * coeff if total is None else total + moved * coeff
    return total


def filters(ar_ref, ma_ref, aro_ref, mao_ref, ids, pt_ref):
    n = ids.shape[1]
    lane = lax.broadcasted_iota(jnp.int32, (1, n), 1)

    def lagged(v, k):
        return v if k == 0 else jnp.where(lane >= k, pltpu.roll(v, k, 1), 0.0)

    impulse = jnp.where(lane == 0, 1.0, 0.0).astype(jnp.float32)
    grid = jnp.broadcast_to(ids, (n, n))
    row = lax.broadcasted_iota(jnp.int32, (n, n), 0)
    col = lax.broadcasted_iota(jnp.int32, (n, n), 1)
    joined = (grid == grid.T) & (col >= row)
    out_rows, in_rows, end_rows = [], [], []
    for c in range(3):
        ar = [jnp.where(k < aro_ref[c], ar_ref[c, k], 0.0) for k in range(LAGS)]
        ma = [jnp.where(k < mao_ref[c], ma_ref[c, k], 0.0) for k in range(LAGS)]
        a, b = [1.0] + [0.0] * LAGS, [1.0] + [0.0] * LAGS
        for k in range(LAGS):
            a = [a[0]] + [a[j] - ar[k] * a[j - 1] for j in range(1, LAGS + 1)]
            b = [b[0]] + [b[j] - ma[k] * b[j - 1] for j in range(1, LAGS + 1)]
        h = impulse
        for k in range(LAGS):
            power, m = ar[k], 1
            while m < n:
                h = h + power * lagged(h, m)
                power, m = power * power, 2 * m
        g = h
        for k in range(LAGS):
            g = g - ma[k] * lagged(g, 1)
        for i in range(1, LAGS + 1):
            out_rows.append((c * LAGS + i - 1, lagged(h, i - 1)))
            acc = jnp.zeros_like(g)
            end = jnp.zeros_like(g)
            for m in range(LAGS + 1 - i):
                acc = acc + b[i + m] * lagged(impulse, m) - a[i + m] * lagged(g, m)
                end = end - a[i + m] * jnp.where(lane == n - 1 - m, 1.0, 0.0)
            in_rows.append((c * LAGS + i - 1, acc))
            end_rows.append((c * LAGS + i - 1, end))
        t = jnp.broadcast_to(g, (n, n))
        bit = 1
        while bit < n:
            t = jnp.where((row // bit) % 2 == 1, pltpu.roll(t, bit, 1), t)
            bit *= 2
        pt_ref[c] = jnp.where(joined, t, 0.0)
    ca = rows_of(out_rows, 16, n)
    flip = jnp.where(row + col == n - 1, 1.0, 0.0).astype(jnp.float32)
    ab = dot(rows_of(in_rows, 16, n), flip, NN, HI)
    ends = rows_of(end_rows, 16, n)
    fwd = bands(dot(ca, tall(ends, n), NT, HI))
    bwd = bands(dot(ends, tall(ca, n), NT, HI))
    return ca, ab, fwd, bwd


def spread(block, mask):
    row = lax.broadcasted_iota(jnp.int32, block.shape, 0)
    return jnp.concatenate(
        [jnp.where(row // LAGS == c, block * mask, 0.0) for c in range(3)], axis=1
    )

def kernel(
    T, O, SUB,
    design, ids_in, gaps_in, ar_ref, ma_ref, aro_ref, mao_ref, kaula, precond_in,
    res_in, direc_in,
    image_out, comb_out, scal_out,
    dv, precond, res, direc, packed, high, low,
    right_in, left_in, obs_out, obs_in, ids_all, summ_out, summ_in, pt,
    rs_right_out, rs_left_out, rs_right_in, rs_left_in, applied, image_applied,
    tot_out, tot_in, tot2_out, tot2_in,
    dsem, in_sem, agr_s, agr_r, agl_s, agl_r, ob_s, ob_r, id_s, id_r, su_s, su_r,
    rr_s, rr_r, rl_s, rl_r, t1_s, t1_r, t2_s, t2_r,
):
    me, order = lax.axis_index("tm"), lax.axis_index("order")
    A = T // 2
    rhs, share = packed.shape
    n = ids_in.shape[1]
    piece_len = share // SUB
    blocks = precond.shape[0]

    def tm_at(p):
        p = lax.rem(p + 2 * T, T)
        return jnp.where(p < A, 2 * p, 2 * (T - 1 - p) + 1)

    pos = jnp.where(me % 2 == 0, me // 2, T - 1 - me // 2)
    right, left = {"tm": tm_at(pos + 1)}, {"tm": tm_at(pos - 1)}
    mesh_ids = pl.DeviceIdType.MESH

    def to_tm(k):
        return {"tm": lax.rem(me + k, T)}

    def to_order(k):
        return {"order": lax.rem(order + k, O)}

    def part(h):
        return slice(h * piece_len, (h + 1) * piece_len)

    def load(dist):
        q = tm_at(pos + dist)
        return pltpu.make_async_copy(
            design.at[:, pl.ds(pl.multiple_of(q * share, 128), share)],
            dv.at[dist % T],
            dsem.at[dist % T],
        )

    def remote(src, dst, ssem, rsem, to):
        return pltpu.make_async_remote_copy(
            src_ref=src, dst_ref=dst, send_sem=ssem, recv_sem=rsem,
            device_id=to, device_id_type=mesh_ids,
        )

    get_direc = pltpu.make_async_copy(direc_in.at[:, 0, :], direc, in_sem.at[0])
    get_res = pltpu.make_async_copy(res_in.at[:, 0, :], res, in_sem.at[1])
    get_precond = pltpu.make_async_copy(precond_in, precond, in_sem.at[2])
    get_direc.start()
    barrier = pltpu.get_barrier_semaphore()
    for k in range(1, T):
        pl.semaphore_signal(barrier, inc=1, device_id=to_tm(k), device_id_type=mesh_ids)
    for k in range(1, O):
        pl.semaphore_signal(barrier, inc=1, device_id=to_order(k), device_id_type=mesh_ids)
    arrivals = [0]
    for s in range(1, A):
        arrivals += [-s, s]
    arrivals.append(A)
    load(0).start()
    get_precond.start()
    get_res.start()
    for dist in arrivals[1:]:
        load(dist).start()
    get_direc.wait()
    packed[...] = direc[...].astype(jnp.bfloat16)
    get_precond.wait()
    for m in range(blocks):
        whole = precond[m]
        top = whole.astype(jnp.bfloat16)
        high[m] = top
        low[m] = (whole - top.astype(jnp.float32)).astype(jnp.bfloat16)
    pl.semaphore_wait(barrier, T - 1 + O - 1)

    def rightward(s, h):
        return not (s == A - 1 and SUB == 2 and h == 1)

    def leftward(s, h):
        return s < A - 1 or (SUB == 2 and h == 1)

    def ag(s, h, into, ssem, rsem, to):
        src = packed.at[:, part(h)] if s == 0 else into.at[s - 1, :, part(h)]
        at = s * SUB + h
        return remote(src, into.at[s, :, part(h)], ssem.at[at], rsem.at[at], to)

    def ag_right(s, h):
        return ag(s, h, right_in, agr_s, agr_r, right)

    def ag_left(s, h):
        return ag(s, h, left_in, agl_s, agl_r, left)

    for j in range(SUB):
        if rightward(0, j):
            ag_right(0, j).start()
        if leftward(0, SUB - 1 - j):
            ag_left(0, SUB - 1 - j).start()
    id_copies = [
        remote(ids_in, ids_all.at[k - 1], id_s.at[k - 1], id_r.at[k - 1], to_tm(k))
        for k in range(1, T)
    ]
    for copy in id_copies:
        copy.start()

    load(0).wait()
    obs = dot(packed[...], dv[0], NT)
    ids = ids_in[0:1, :].astype(jnp.float32)
    ca, ab, fwd, bwd = filters(ar_ref, ma_ref, aro_ref, mao_ref, ids, pt)
    for s in range(A):
        for j in range(SUB):
            h, g = j, SUB - 1 - j
            if rightward(s, h):
                ag_right(s, h).wait_recv()
                if s + 1 < A and rightward(s + 1, h):
                    ag_right(s + 1, h).start()
            if leftward(s, g):
                ag_left(s, g).wait_recv()
                if s + 1 < A and leftward(s + 1, g):
                    ag_left(s + 1, g).start()
            if j == 0:
                load((-(s + 1)) % T if s < A - 1 else A).wait()
                if s < A - 1:
                    load(s + 1).wait()
            if rightward(s, h):
                obs = obs + dot(right_in[s, :, part(h)], dv[(-(s + 1)) % T, :, part(h)], NT)
            if leftward(s, g):
                obs = obs + dot(left_in[s, :, part(g)], dv[s + 1, :, part(g)], NT)
    obs_out[...] = obs
    ob_copies = [
        remote(obs_out, obs_in.at[k - 1], ob_s.at[k - 1], ob_r.at[k - 1], to_order(k))
        for k in range(1, O)
    ]
    for copy in ob_copies:
        copy.start()

    first, last = ids[:, 0:1], ids[:, n - 1 : n]
    at_first = jnp.where(ids == first, 1.0, 0.0)
    at_last = jnp.where(ids == last, 1.0, 0.0)
    head_map = spread(ca, at_first)
    tail_map = spread(ab, at_last)
    head_map = jnp.concatenate(
        [dot(head_map[:, c * n : (c + 1) * n], pt[c], NT, HI) for c in range(3)], axis=1
    )
    state_map = jnp.concatenate([tall(tail_map, n // 2), tall(head_map, n // 2)], axis=0)
    for copy in id_copies:
        copy.wait_recv()
    ids_e = []
    for e in range(T):
        slot = jnp.minimum(lax.rem(me - e + T - 1, T), T - 2)
        ids_e.append(jnp.where(me == e, ids, ids_all[slot].astype(jnp.float32)))
    firsts = [v[:, 0:1] for v in ids_e]
    lasts = [v[:, n - 1 : n] for v in ids_e]
    runs = jnp.concatenate(
        [ca * jnp.where(v == f, 1.0, 0.0) for v, f in zip(ids_e, firsts)], axis=0
    )
    energy = dot(runs, tall(ca, n), NT, HI)
    energies = [bands(energy[16 * e : 16 * e + 16]) for e in range(T)]

    for copy in ob_copies:
        copy.wait_recv()
    for k in range(1, O):
        obs = obs + obs_in[k - 1]
    gaps3 = jnp.concatenate([gaps_in[0:1, :].astype(jnp.float32)] * 3, axis=1)
    masked = obs * gaps3
    summary = dot(masked, state_map, NT, HI)
    summ_out[...] = summary
    su_copies = [
        remote(summ_out, summ_in.at[k - 1], su_s.at[k - 1], su_r.at[k - 1], to_tm(k))
        for k in range(1, T)
    ]
    for copy in su_copies:
        copy.start()
    local_back = jnp.concatenate(
        [
            dot(dot(masked[:, c * n : (c + 1) * n], pt[c], NN, HI), pt[c], NT, HI)
            for c in range(3)
        ],
        axis=1,
    )

    def preconditioned(v, cols):
        out = []
        for m in range(cols.start // 128, cols.stop // 128):
            x = v[:, m * 128 - cols.start : (m + 1) * 128 - cols.start]
            top = x.astype(jnp.bfloat16)
            rest = (x - top.astype(jnp.float32)).astype(jnp.bfloat16)
            both = dot(jnp.concatenate([top, rest], axis=0), high[m], NT)
            out.append(both[:rhs] + both[rhs:] + dot(top, low[m], NT))
        return jnp.concatenate(out, axis=1)

    get_res.wait()
    applied[...] = preconditioned(res[...], slice(0, share))
    for copy in su_copies:
        copy.wait_recv()
    sums = []
    for e in range(T):
        slot = jnp.minimum(lax.rem(me - e + T - 1, T), T - 2)
        sums.append(jnp.where(me == e, summary, summ_in[slot]))
    state = jnp.zeros_like(summary)
    mine_in = jnp.zeros_like(summary)
    ins = []
    for e in range(T):
        entering = state if e == 0 else state * jnp.where(lasts[e - 1] == firsts[e], 1.0, 0.0)
        ins.append(entering)
        mine_in = jnp.where(me == e, entering, mine_in)
        through = jnp.where(firsts[e] == lasts[e], 1.0, 0.0)
        state = sums[e] + through * banded(entering, fwd)
    back = jnp.zeros_like(summary)
    mine_back = jnp.zeros_like(summary)
    for e in range(T - 1, 0, -1):
        through = jnp.where(firsts[e] == lasts[e], 1.0, 0.0)
        heads = pltpu.roll(sums[e], n // 2, 1) + banded(ins[e], energies[e])
        back = (heads + through * banded(back, bwd)) * jnp.where(
            lasts[e - 1] == firsts[e], 1.0, 0.0
        )
        mine_back = jnp.where(me == e - 1, back, mine_back)
    lane = lax.broadcasted_iota(jnp.int32, summary.shape, 1)
    states = jnp.where(lane < n // 2, mine_back, pltpu.roll(mine_in, n // 2, 1))
    adjoint = local_back + dot(states, state_map, NN, HI)
    weighted = (adjoint * gaps3).astype(jnp.bfloat16)

    def grad(dist, h):
        return dot(weighted, dv[dist % T, :, part(h)], NN)

    def rs_right(s, h):
        at = s * SUB + h
        return remote(
            rs_right_out.at[s, :, part(h)], rs_right_in.at[s, :, part(h)],
            rr_s.at[at], rr_r.at[at], right,
        )

    def rs_left(s, h):
        at = s * SUB + h
        return remote(
            rs_left_out.at[s, :, part(h)], rs_left_in.at[s, :, part(h)],
            rl_s.at[at], rl_r.at[at], left,
        )

    def sends_right(s, h):
        return rightward(A - 1 - s, h)

    def sends_left(s, h):
        return leftward(A - 1 - s, h)

    for s in range(A):
        for j in range(SUB):
            h, g = j, SUB - 1 - j
            if sends_right(s, h):
                piece = grad(A - s, h)
                if s > 0 and sends_right(s - 1, h):
                    rs_right(s - 1, h).wait_recv()
                    piece = piece + rs_right_in[s - 1, :, part(h)].astype(jnp.float32)
                rs_right_out[s, :, part(h)] = piece.astype(LINK)
                rs_right(s, h).start()
            if sends_left(s, g):
                piece = grad(s - A, g)
                if s > 0 and sends_left(s - 1, g):
                    rs_left(s - 1, g).wait_recv()
                    piece = piece + rs_left_in[s - 1, :, part(g)].astype(jnp.float32)
                rs_left_out[s, :, part(g)] = piece.astype(LINK)
                rs_left(s, g).start()
    owns = [grad(0, h) for h in range(SUB)]
    images = []
    for h in range(SUB):
        own = owns[h] + kaula[:, part(h)] * direc[:, part(h)]
        if sends_right(A - 1, h):
            rs_right(A - 1, h).wait_recv()
            own = own + rs_right_in[A - 1, :, part(h)].astype(jnp.float32)
        if sends_left(A - 1, h):
            rs_left(A - 1, h).wait_recv()
            own = own + rs_left_in[A - 1, :, part(h)].astype(jnp.float32)
        images.append(own)
        image_applied[:, part(h)] = preconditioned(own, part(h))
    image = jnp.concatenate(images, axis=1)
    image_out[...] = image
    app, imapp = applied[...], image_applied[...]
    d, r = direc[...], res[...]
    lane = lax.broadcasted_iota(jnp.int32, (rhs, 128), 1)
    row = lax.broadcasted_iota(jnp.int32, (rhs, 128), 0)
    products = [r * app, d * image, image * app, image * imapp]
    total = jnp.zeros((rhs, 128), jnp.float32)
    for q, product in enumerate(products):
        total = jnp.where(lane == q * rhs + row, jnp.sum(product, axis=1, keepdims=True), total)
    total = jnp.broadcast_to(jnp.sum(total, axis=0, keepdims=True), (8, 128))

    def gather_sum(value, out, into, ssem, rsem, count, to):
        out[...] = value
        copies = [
            remote(out, into.at[k - 1], ssem.at[k - 1], rsem.at[k - 1], to(k))
            for k in range(1, count)
        ]
        for copy in copies:
            copy.start()
        for k, copy in enumerate(copies):
            copy.wait_recv()
            value = value + into[k]
        return value, copies

    total, c1 = gather_sum(total, tot_out, tot_in, t1_s, t1_r, O, to_order)
    total, c2 = gather_sum(total, tot2_out, tot2_in, t2_s, t2_r, T, to_tm)
    wide = jnp.broadcast_to(total[0:1, :], (rhs, 128))
    old_rz, curvature, cross, quad = [
        jnp.sum(jnp.where(lane == q * rhs + row, wide, 0.0), axis=1, keepdims=True)
        for q in range(4)
    ]
    step = old_rz / curvature
    new_rz = old_rz - 2.0 * step * cross + step * step * quad
    comb_out[...] = app - step * imapp
    scal_out[...] = jnp.where(lane == 0, step, new_rz / old_rz)

    for s in range(A):
        for h in range(SUB):
            if rightward(s, h):
                ag_right(s, h).wait_send()
            if leftward(s, h):
                ag_left(s, h).wait_send()
            if sends_right(s, h):
                rs_right(s, h).wait_send()
            if sends_left(s, h):
                rs_left(s, h).wait_send()
    for copy in id_copies + ob_copies + su_copies + c1 + c2:
        copy.wait_send()


def finish(image, comb, scal, sol, res, direc, new_sol, new_res, new_dir, got, put, isem, osem):
    def fetch(k, ref):
        return pltpu.make_async_copy(ref.at[:, 0, :], got.at[k], isem.at[k])

    def store(k, ref):
        return pltpu.make_async_copy(put.at[k], ref.at[:, 0, :], osem.at[k])

    for k, ref in ((2, direc), (0, sol), (1, res)):
        fetch(k, ref).start()
    step, ratio = scal[:, 0:1], scal[:, 1:2]
    fetch(2, direc).wait()
    put[2] = comb[...] + ratio * got[2]
    store(2, new_dir).start()
    fetch(0, sol).wait()
    put[0] = got[0] + step * got[2]
    store(0, new_sol).start()
    fetch(1, res).wait()
    put[1] = got[1] - step * image[...]
    store(1, new_res).start()
    for k, ref in ((2, new_dir), (0, new_sol), (1, new_res)):
        store(k, ref).wait()


def on_device(
    T, O, design, gap_flags, segment_ids, ar_order, ma_order, ar_roots, ma_roots,
    kaula, precond, solution, residual, direction,
):
    n = segment_ids.shape[0]
    columns = design.shape[2]
    share = direction.shape[2]
    rhs = direction.shape[0]
    blocks = precond.shape[1]
    f32, bf16 = jnp.float32, jnp.bfloat16
    SUB = 2 if share % 256 == 0 else 1
    A = T // 2
    vmem = pl.BlockSpec(memory_space=pltpu.VMEM)
    smem = pl.BlockSpec(memory_space=pltpu.SMEM)
    hbm = pl.BlockSpec(memory_space=pl.ANY)
    V, D = pltpu.VMEM, lambda k: pltpu.SemaphoreType.DMA((max(k, 1),))
    vec = jax.ShapeDtypeStruct((rhs, share), f32)
    image, comb, scal = pl.pallas_call(
        functools.partial(kernel, T, O, SUB),
        out_shape=[vec, vec, jax.ShapeDtypeStruct((rhs, 128), f32)],
        in_specs=[hbm, vmem, vmem, smem, smem, smem, smem, vmem, hbm, hbm, hbm],
        out_specs=[vmem] * 3,
        scratch_shapes=[
            V((T, 3 * n, share), bf16), V((blocks, 128, 128), f32), V((rhs, share), f32),
            V((rhs, share), f32), V((rhs, share), bf16), V((blocks, 128, 128), bf16),
            V((blocks, 128, 128), bf16),
            V((A, rhs, share), bf16), V((A, rhs, share), bf16),
            V((rhs, 3 * n), f32), V((O - 1, rhs, 3 * n), f32), V((T - 1, 1, n), jnp.int32),
            V((rhs, n), f32), V((T - 1, rhs, n), f32), V((3, n, n), f32),
            V((A, rhs, share), LINK), V((A, rhs, share), LINK),
            V((A, rhs, share), LINK), V((A, rhs, share), LINK),
            V((rhs, share), f32), V((rhs, share), f32),
            V((8, 128), f32), V((O - 1, 8, 128), f32), V((8, 128), f32), V((T - 1, 8, 128), f32),
            D(T), D(3), D(A * SUB), D(A * SUB), D(A * SUB), D(A * SUB), D(O - 1), D(O - 1),
            D(T - 1), D(T - 1), D(T - 1), D(T - 1), D(A * SUB), D(A * SUB), D(A * SUB),
            D(A * SUB), D(O - 1), D(O - 1), D(T - 1), D(T - 1),
        ],
        compiler_params=pltpu.CompilerParams(
            collective_id=0, has_side_effects=True, vmem_limit_bytes=56 * 1024 * 1024
        ),
    )(
        design.reshape(3 * n, columns), segment_ids.reshape(1, n), gap_flags.reshape(1, n),
        ar_roots, ma_roots, ar_order, ma_order, kaula, precond[0], residual, direction,
    )
    full = jax.ShapeDtypeStruct(direction.shape, f32)
    return tuple(
        pl.pallas_call(
            finish,
            out_shape=[full] * 3,
            in_specs=[vmem, vmem, vmem, hbm, hbm, hbm],
            out_specs=[hbm] * 3,
            scratch_shapes=[V((3, rhs, share), f32), V((3, rhs, share), f32), D(3), D(3)],
        )(image, comb, scal, solution, residual, direction)
    )


def solution(mesh):
    vec = P(None, "order", "tm")
    in_specs = (
        P(None, "tm", "order"), P("tm"), P("tm"), P(), P(), P(), P(), P("order", "tm"),
        P("order", "tm", None, None), vec, vec, vec,
    )
    body = functools.partial(on_device, mesh.shape["tm"], mesh.shape["order"])
    return jax.shard_map(
        body, mesh=mesh, in_specs=in_specs, out_specs=(vec, vec, vec), check_vma=False
    )
```
